32 devices in a mesh: gx: 4 (over y, x), gy: 8 (over z, core).
Axes of the slice: x: 2, y: 2, z: 4, core: 2. Of those that a mesh axis runs over, the one named last changes fastest.
Arguments:
- vol_rhs: float32 [2, 120, 32768], P(None, None, ('gx', 'gy')), may hold values from -6 to 6
- trace_in: float32 [2, 36, 65536], P(None, None, ('gx', 'gy')), may hold values from -6 to 6
- pml_flag: int32 [32768], P(('gx', 'gy')), may hold values 0 or 1
- stretch: float32 [32768], P(('gx', 'gy')), may hold values from 0.5 to 4
- cond_op: float32 [4, 2, 36, 120], replicated, may hold values from -0.375 to 0.375
- skel_op: float32 [7, 2, 36, 36], replicated, may hold values from -1 to 4
- block_coef: float32 [7, 2, 65536], P(None, None, ('gx', 'gy')), may hold values from -27 to 27
- recon_op: float32 [2, 120, 120], replicated, may hold values from -0.375 to 0.375
- lift_op: float32 [4, 2, 120, 36], replicated, may hold values from -0.375 to 0.375
- elem_face: int32 [4, 32768], P(None, ('gx', 'gy')), may hold values from 0 to 4095, as said below
- adjacency: int32 [6, 65536], P(None, ('gx', 'gy')), may hold values from -1 to 4095, as said below
- halo_list: int32 [8, 8192], P(None, ('gx', 'gy')), may hold values from -1 to 2047, as said below
Outputs:
- trace_out: float32 [2, 36, 65536], P(None, None, ('gx', 'gy'))
- volume_out: float32 [2, 120, 32768], P(None, None, ('gx', 'gy'))
The draws below stay inside these ranges and needn't reach their ends.
Inputs may be any that keep to these rules, and one draw needn't show every extreme that they name: The list of direction d of partition p is halo_list[d, p * 256 .. (p + 1) * 256 - 1], local face numbers of p: its live entries are distinct and come first, -1 fills the rest; lists towards a position outside the grid are empty; in every draw some list is full. `elem_face`: every ghost slot named is a live entry of the list of an existing partition. `adjacency`: every ghost slot named is a live entry of the list of an existing partition; each face has 3 or 6 live entries, first, then -1.
All inputs are finite; a program needn't handle non-finite values. No bound on the sum of `pml_flag` on one device may be relied on, other than what follows from the above.
Results may differ from the reference program's by a relative error of at most 0.0003.
Values sent between devices are 32-bit elements; how exact they have to be, the bound alone decides.
A program may use at most 128 MiB of HBM per device.

```python
import math
import jax
import jax.numpy as jnp
from jax import lax

NQ = 36
NV = 120
NADJ = 6
DIRS = 8
E_DEV = 1024
F_DEV = 2048
HALO = 256
ELEMS = 32768
FACES = 65536
N_GX = 4
N_GY = 8
DEVICES = 32


OFFSETS = ((-1, -1), (-1, 0), (-1, 1), (0, -1), (0, 1), (1, -1), (1, 0), (1, 1))


def offset_tables():
    return (jnp.array([entry[0] for entry in OFFSETS], jnp.int32), jnp.array([entry[1] for entry in OFFSETS], jnp.int32))


def halo_counts(key):
    shift_x, shift_y = offset_tables()
    device = jnp.arange(DEVICES, dtype=jnp.int32)
    target_x = (device // N_GY)[:, None] + shift_x[None, :]
    target_y = (device % N_GY)[:, None] + shift_y[None, :]
    exists = (target_x >= 0) & (target_x < N_GX) & (target_y >= 0) & (target_y < N_GY)
    counts = jax.random.randint(jax.random.fold_in(key, 11), (DEVICES, DIRS), HALO // 4, HALO + 1)
    chosen = jax.random.randint(jax.random.fold_in(key, 12), (), 0, DEVICES)
    counts = jnp.where(device[:, None] == chosen, HALO, counts)
    return jnp.where(exists, counts, 0)


def draw_targets(key, salt, entries):
    counts = halo_counts(key)
    shift_x, shift_y = offset_tables()
    subkeys = jax.random.split(jax.random.fold_in(key, salt), 4)
    device = jnp.arange(DEVICES, dtype=jnp.int32)[:, None]
    local_pick = jax.random.randint(subkeys[0], (DEVICES, entries), 0, F_DEV)
    direction = jax.random.randint(subkeys[1], (DEVICES, entries), 0, DIRS)
    sender_x = device // N_GY - shift_x[direction]
    sender_y = device % N_GY - shift_y[direction]
    inside = (sender_x >= 0) & (sender_x < N_GX) & (sender_y >= 0) & (sender_y < N_GY)
    sender = jnp.clip(sender_x, 0, N_GX - 1) * N_GY + jnp.clip(sender_y, 0, N_GY - 1)
    available = jnp.where(inside, counts[sender, direction], 0)
    position = jax.random.randint(subkeys[2], (DEVICES, entries), 0, 1 << 20) % jnp.maximum(available, 1)
    use_ghost = (jax.random.randint(subkeys[3], (DEVICES, entries), 0, 10) < 3) & (available > 0)
    return jnp.where(use_ghost, F_DEV + direction * HALO + position, local_pick)


def draw_elem_face(key, part):
    targets = draw_targets(key, 21, 4 * E_DEV).reshape(DEVICES, 4, E_DEV)
    return targets.transpose(1, 0, 2).reshape(4, ELEMS).astype(jnp.int32)


def draw_adjacency(key, part):
    targets = draw_targets(key, 31, NADJ * F_DEV).reshape(DEVICES, NADJ, F_DEV)
    boundary_face = jax.random.randint(jax.random.fold_in(key, 32), (DEVICES, 1, F_DEV), 0, 5) == 0
    live_count = jnp.where(boundary_face, 3, NADJ)
    slot_rank = jnp.arange(NADJ, dtype=jnp.int32)[None, :, None]
    padded_targets = jnp.where(slot_rank < live_count, targets, -1)
    return padded_targets.transpose(1, 0, 2).reshape(NADJ, FACES).astype(jnp.int32)


def draw_prefix(subkey):
    return jax.random.permutation(subkey, F_DEV)[:HALO]


def draw_halo_list(key, part):
    counts = halo_counts(key)
    subkeys = jax.random.split(jax.random.fold_in(key, 13), DEVICES * DIRS)
    chosen_faces = jax.vmap(draw_prefix)(subkeys).reshape(DEVICES, DIRS, HALO)
    is_live = jnp.arange(HALO, dtype=jnp.int32)[None, None, :] < counts[:, :, None]
    halo_rows = jnp.where(is_live, chosen_faces, -1)
    return halo_rows.transpose(1, 0, 2).reshape(DIRS, DEVICES * HALO).astype(jnp.int32)


def draw_skel_op(key, part):
    noise = jnp.clip(jax.random.normal(key, (NADJ + 1, 2, NQ, NQ), jnp.float32), -4.0, 4.0)
    scaled = noise * NQ ** (-0.5)
    centre = 3.0 * jnp.eye(NQ, dtype=jnp.float32) + 0.25 * noise[0, 0]
    return scaled.at[0, 0].set(centre).at[0, 1].set(0.25 * noise[0, 1])


def draw_block_coef(key, part):
    subkeys = jax.random.split(key, 2)
    device = (jnp.arange(FACES, dtype=jnp.int32) // F_DEV).astype(jnp.float32)
    level = device / max(DEVICES - 1, 1)
    magnitude = jnp.exp(jax.random.uniform(subkeys[0], (NADJ + 1, FACES), jnp.float32, jnp.log(0.5), jnp.log(2.0)))
    rising = 3.0 ** level
    phase = jax.random.uniform(subkeys[1], (NADJ + 1, FACES), jnp.float32, -3.14159, 3.14159)
    phase = phase.at[0].multiply(0.15)
    size_all = magnitude * rising[None, :]
    return jnp.stack([size_all * jnp.cos(phase), size_all * jnp.sin(phase)], axis=1)


def with_ends(drawn, stream_key, low, high):
    place = [jax.random.randint(jax.random.fold_in(stream_key, axis), (), 0, length) for axis, length in enumerate(drawn.shape)]
    longest = drawn.shape.index(max(drawn.shape))
    beside = place[:longest] + [(place[longest] + 1) % drawn.shape[longest]] + place[longest + 1:]
    return drawn.at[tuple(place)].set(low).at[tuple(beside)].set(high)


def level_of(rng, dims, cuts, low, top_value):
    gain = 1.0
    for dim, blocks in cuts:
        steps = jax.random.uniform(jax.random.fold_in(jax.random.fold_in(rng, 6), dim), (blocks,), jnp.float32, low / len(cuts), top_value / len(cuts))
        gain = gain * jnp.repeat(jnp.exp(steps), dims[dim] // blocks).reshape((-1,) + (1,) * (len(dims) - 1 - dim))
    return gain


def gaussian(stream_key, dims, width, bound, shards=(), kind=jnp.bfloat16):
    values = jax.random.normal(stream_key, dims, jnp.float32) * width
    if len(shards) > 0:
        values = level_of(stream_key, dims, shards, -0.22, 0.18) * values
    return jnp.clip(values, min=-bound, max=bound).astype(kind)


def setup_inputs(seed: int = 0) -> dict:
    splits = jax.random.split(jax.random.key(seed), 13)
    return {
        "vol_rhs": gaussian(splits[0], (2, NV, ELEMS), 1.0, 6.0, ((2, 32),), jnp.float32),
        "trace_in": gaussian(splits[1], (2, NQ, FACES), 1.0, 6.0, ((2, 32),), jnp.float32),
        "pml_flag": with_ends((jax.random.randint(splits[2], (ELEMS,), 0, 3) < 1).astype(jnp.int32), jax.random.fold_in(splits[2], 1), 0, 1),
        "stretch": jnp.clip(jnp.exp(math.log(4.0) - 2.0794415 * jax.random.uniform(splits[3], (ELEMS,), jnp.float32) ** level_of(splits[3], (ELEMS,), ((0, 32),), -0.2, 0.2)), 0.5, 4.0),
        "cond_op": gaussian(splits[4], (4, 2, NQ, NV), (2 * NV) ** -0.5, 0.375, (), jnp.float32),
        "skel_op": draw_skel_op(jax.random.fold_in(splits[12], 71), 0),
        "block_coef": draw_block_coef(jax.random.fold_in(splits[12], 71), 0),
        "recon_op": gaussian(splits[7], (2, NV, NV), (2 * NV) ** -0.5, 0.375, (), jnp.float32),
        "lift_op": gaussian(splits[8], (4, 2, NV, NQ), (8 * NQ) ** -0.5, 0.375, (), jnp.float32),
        "elem_face": draw_elem_face(jax.random.fold_in(splits[12], 71), 0),
        "adjacency": draw_adjacency(jax.random.fold_in(splits[12], 71), 0),
        "halo_list": draw_halo_list(jax.random.fold_in(splits[12], 71), 0),
    }


OFFSETS = ((-1, -1), (-1, 0), (-1, 1), (0, -1), (0, 1), (1, -1), (1, 0), (1, 1))


def complex_block(complex_pair):
    top_row = jnp.concatenate([complex_pair[0], -complex_pair[1]], axis=1)
    bottom_row = jnp.concatenate([complex_pair[1], complex_pair[0]], axis=1)
    return jnp.concatenate([top_row, bottom_row], axis=0)


def complex_scale(scale_real, scale_imag, vector):
    half_rows = vector.shape[-2] // 2
    real_part = vector[..., :half_rows, :]
    imag_part = vector[..., half_rows:, :]
    return jnp.concatenate([scale_real * real_part - scale_imag * imag_part, scale_real * imag_part + scale_imag * real_part], axis=-2)


def apply_matrix(matrix, batched):
    return jnp.einsum("ij,pjn->pin", matrix, batched, precision=lax.Precision.HIGHEST)


def take_columns(values, columns):
    clipped = jnp.maximum(columns, 0)
    picked = jax.vmap(lambda source, wanted: source[:, wanted])(values, clipped)
    return jnp.where(columns[:, None, :] >= 0, picked, 0.0)


def add_columns(target, columns, values):
    return target.at[:, columns].add(values)


def grid_shift(blocks, step_x, step_y):
    grid_view = blocks.reshape((N_GX, N_GY) + blocks.shape[1:])
    widths = ((1, 1), (1, 1)) + ((0, 0),) * (blocks.ndim - 1)
    padded = jnp.pad(grid_view, widths)
    moved = padded[1 - step_x:1 - step_x + N_GX, 1 - step_y:1 - step_y + N_GY]
    return moved.reshape(blocks.shape)


def per_device(array, rows):
    return array.reshape(rows, DEVICES, -1).transpose(1, 0, 2)


def to_global(batched, shape):
    return batched.transpose(1, 0, 2).reshape(shape)


def with_ghosts(own_faces, lists):
    outgoing = take_columns(own_faces, lists.reshape(DEVICES, DIRS * HALO))
    outgoing = outgoing.reshape(DEVICES, own_faces.shape[1], DIRS, HALO)
    arrived = [grid_shift(outgoing[:, :, direction], OFFSETS[direction][0], OFFSETS[direction][1]) for direction in range(DIRS)]
    return jnp.concatenate([own_faces] + arrived, axis=2)


def owner_sum(collected, lists):
    own_faces = collected[:, :, :F_DEV]
    for direction in range(DIRS):
        offset_at = F_DEV + direction * HALO
        returned = grid_shift(collected[:, :, offset_at:offset_at + HALO], -OFFSETS[direction][0], -OFFSETS[direction][1])
        columns = lists[:, direction]
        returned = jnp.where(columns[:, None, :] >= 0, returned, 0.0)
        own_faces = jax.vmap(add_columns)(own_faces, jnp.maximum(columns, 0), returned)
    return own_faces


def reference(vol_rhs, trace_in, pml_flag, stretch, cond_op, skel_op, block_coef, recon_op, lift_op, elem_face, adjacency, halo_list):
    trace_rows = 2 * NQ
    volume = per_device(vol_rhs, 2 * NV)
    traces = per_device(trace_in, trace_rows)
    pml_tilt = (pml_flag.astype(jnp.float32) * stretch).reshape(DEVICES, 1, E_DEV)
    lists = halo_list.reshape(DIRS, DEVICES, HALO).transpose(1, 0, 2)
    slots = elem_face.reshape(4, DEVICES, E_DEV).transpose(1, 0, 2).reshape(DEVICES, 4 * E_DEV)
    neighbours = adjacency.reshape(NADJ, DEVICES, F_DEV).transpose(1, 0, 2)
    coefficient = block_coef.reshape(NADJ + 1, 2, DEVICES, F_DEV).transpose(2, 0, 1, 3)
    cond_big = jnp.concatenate([complex_block(cond_op[corner]) for corner in range(4)], axis=0)
    pieces = apply_matrix(cond_big, volume).reshape(DEVICES, 4, trace_rows, E_DEV)
    pieces = complex_scale(1.0, pml_tilt[:, None], pieces)
    flat_pieces = pieces.transpose(0, 2, 1, 3).reshape(DEVICES, trace_rows, 4 * E_DEV)
    collected = jnp.zeros((DEVICES, trace_rows, F_DEV + DIRS * HALO), jnp.float32)
    collected = jax.vmap(add_columns)(collected, slots, flat_pieces)
    rhs_skeleton = owner_sum(collected, lists)
    skel_blocks = [complex_block(skel_op[block_number]) for block_number in range(NADJ + 1)]

    def skeleton(own_faces):
        extended = with_ghosts(own_faces, lists)
        result = complex_scale(coefficient[:, 0, 0:1], coefficient[:, 0, 1:2], apply_matrix(skel_blocks[0], own_faces))
        for neighbour in range(NADJ):
            gathered = take_columns(extended, neighbours[:, neighbour])
            product = apply_matrix(skel_blocks[neighbour + 1], gathered)
            result = result + complex_scale(coefficient[:, neighbour + 1, 0:1], coefficient[:, neighbour + 1, 1:2], product)
        return result

    residual_now = rhs_skeleton - skeleton(traces)
    image = skeleton(residual_now)
    image_real = image[:, :NQ]
    image_imag = image[:, NQ:]
    residual_real = residual_now[:, :NQ]
    residual_imag = residual_now[:, NQ:]
    numer_real = jnp.sum(image_real * residual_real + image_imag * residual_imag)
    numer_imag = jnp.sum(image_real * residual_imag - image_imag * residual_real)
    power_sum = jnp.sum(image * image)
    step_real = numer_real / power_sum
    step_imag = numer_imag / power_sum
    trace_new = traces + complex_scale(step_real, step_imag, residual_now)
    extended = with_ghosts(trace_new, lists)
    picked = take_columns(extended, slots).reshape(DEVICES, trace_rows, 4, E_DEV)
    picked = picked.transpose(0, 2, 1, 3).reshape(DEVICES, 4 * trace_rows, E_DEV)
    lift_big = jnp.concatenate([complex_block(lift_op[corner]) for corner in range(4)], axis=1)
    volume_new = complex_scale(1.0, pml_tilt, apply_matrix(complex_block(recon_op), volume)) - apply_matrix(lift_big, picked)
    return to_global(trace_new, (2, NQ, FACES)), to_global(volume_new, (2, NV, ELEMS))
```

```python
import functools

import jax
import jax.numpy as jnp
from jax import lax
from jax.experimental import pallas as pl
from jax.experimental.pallas import tpu as pltpu
from jax.sharding import PartitionSpec as P

OFFSETS = ((-1, -1), (-1, 0), (-1, 1), (0, -1), (0, 1), (1, -1), (1, 0), (1, 1))
LANES = 128
TILE = 256
MESH = pl.DeviceIdType.MESH
VMEM = pl.BlockSpec(memory_space=pltpu.VMEM)
SMEM = pl.BlockSpec(memory_space=pltpu.SMEM)
BIG = 60 * 1024 * 1024


def complex_block(complex_pair):
    top_row = jnp.concatenate([complex_pair[0], -complex_pair[1]], axis=1)
    bottom_row = jnp.concatenate([complex_pair[1], complex_pair[0]], axis=1)
    return jnp.concatenate([top_row, bottom_row], axis=0)


def times_i(rows):
    half = rows.shape[-1] // 2
    return jnp.concatenate([-rows[..., half:], rows[..., :half]], axis=-1)


def pad_lanes(rows):
    return jnp.pad(rows, ((0, 0),) * (rows.ndim - 1) + ((0, LANES - rows.shape[-1]),))


def split(x):
    high = x.astype(jnp.bfloat16)
    return high, (x - high.astype(jnp.float32)).astype(jnp.bfloat16)


def gather_rows(source, index, index_base, target, count, group=32):
    @pl.loop(0, count // group)
    def _(step):
        base = step * group
        rows = [source[pl.ds(index[index_base + base + u], 1), :] for u in range(group)]
        for u in range(group):
            target[pl.ds(base + u, 1), :] = rows[u]


def scatter_kernel(slot, lists, pieces, own, collected, parcels, part0, part1, part2):
    count = pieces.shape[0] // 4
    parts = (collected, part0, part1, part2)
    for part in parts:
        part[...] = jnp.zeros_like(part)

    @pl.loop(0, count // 8)
    def _(step):
        for u in range(8):
            e = step * 8 + u
            places = [slot[corner * count + e] for corner in range(4)]
            sums = [
                parts[corner][pl.ds(places[corner], 1), :] + pieces[pl.ds(corner * count + e, 1), :]
                for corner in range(4)
            ]
            for corner in range(4):
                parts[corner][pl.ds(places[corner], 1), :] = sums[corner]

    gather_rows(own, lists, 0, parcels, parcels.shape[0])

    @pl.loop(0, collected.shape[0] // TILE)
    def _(step):
        rows = pl.ds(pl.multiple_of(step * TILE, TILE), TILE)
        collected[rows, :] = (collected[rows, :] + part0[rows, :]) + (part1[rows, :] + part2[rows, :])


def apply_skeleton(adjacent, extended, coef, weights, gathered, finish):
    faces = coef.shape[0]
    neighbours = gathered.shape[0]

    @pl.loop(0, faces // TILE)
    def _(step):
        base = pl.multiple_of(step * TILE, TILE)

        @pl.loop(0, TILE // 8)
        def _(group):
            first = group * 8
            for k in range(neighbours):
                rows = [
                    extended[pl.ds(adjacent[k * faces + base + first + u], 1), :] for u in range(8)
                ]
                for u in range(8):
                    gathered[k, pl.ds(first + u, 1), :] = rows[u]

        scale = coef[pl.ds(base, TILE), :]
        total = None
        for k in range(neighbours + 1):
            x = extended[pl.ds(base, TILE), :] if k == 0 else gathered[k - 1]
            both = jnp.concatenate(split(x), axis=1)
            y = jnp.dot(both, weights[k, 0], preferred_element_type=jnp.float32)
            y += jnp.dot(both, weights[k, 1], preferred_element_type=jnp.float32)
            term = scale[:, 2 * k : 2 * k + 1] * y[:, :LANES] + scale[:, 2 * k + 1 : 2 * k + 2] * y[:, LANES:]
            total = term if total is None else total + term
        finish(base, total)


def residual_kernel(
    adjacent, lists, owners, coef, weights, own, ghost, collected, returned,
    residual, parcels, extended, gathered, sums,
):
    faces = own.shape[0]
    extended[:faces, :] = own[...]
    extended[faces:, :] = ghost[...]
    sums[:faces, :] = collected[...]

    @pl.loop(0, returned.shape[0] // 16)
    def _(step):
        places = [owners[step * 16 + u] for u in range(16)]
        rows = [
            sums[pl.ds(places[u], 1), :] + returned[pl.ds(step * 16 + u, 1), :] for u in range(16)
        ]
        for u in range(16):
            sums[pl.ds(places[u], 1), :] = rows[u]

    def finish(base, total):
        residual[pl.ds(base, TILE), :] = sums[pl.ds(base, TILE), :] - total

    apply_skeleton(adjacent, extended, coef, weights, gathered, finish)
    gather_rows(residual, lists, 0, parcels, parcels.shape[0])


def image_kernel(half, adjacent, slot, coef, weights, own, ghost, partial, picked, extended, gathered):
    faces = own.shape[0]
    extended[:faces, :] = own[...]
    extended[faces:, :] = ghost[...]
    partial[...] = jnp.zeros_like(partial)
    lane = lax.broadcasted_iota(jnp.int32, (TILE, LANES), 1)

    def finish(base, total):
        res = extended[pl.ds(base, TILE), :]
        down = pltpu.roll(res, LANES - half, 1)
        up = pltpu.roll(res, half, 1)
        turned = jnp.where(lane < half, down, -up)
        partial[0:1, :] += jnp.sum(total * res, axis=0, keepdims=True)
        partial[1:2, :] += jnp.sum(total * turned, axis=0, keepdims=True)
        partial[2:3, :] += jnp.sum(total * total, axis=0, keepdims=True)

    apply_skeleton(adjacent, extended, coef, weights, gathered, finish)
    gather_rows(extended, slot, 0, picked, picked.shape[0])


def pick_kernel(slot, own, ghost, picked, extended):
    faces = own.shape[0]
    extended[:faces, :] = own[...]
    extended[faces:, :] = ghost[...]
    gather_rows(extended, slot, 0, picked, picked.shape[0])


def exchange_kernel(signs, n_gx, n_gy, *refs):
    count = len(signs)
    sources, targets = refs[:count], refs[count : 2 * count]
    send_sem, recv_sem = refs[2 * count :]
    here_x, here_y = lax.axis_index("gx"), lax.axis_index("gy")

    def inside(off, sign):
        x, y = here_x + sign * off[0], here_y + sign * off[1]
        return (x >= 0) & (x < n_gx) & (y >= 0) & (y < n_gy)

    barrier = pltpu.get_barrier_semaphore()
    for off in OFFSETS:

        @pl.when(inside(off, 1))
        def _():
            pl.semaphore_signal(
                barrier, inc=1, device_id=(here_x + off[0], here_y + off[1]), device_id_type=MESH
            )

    peers = 0
    for off in OFFSETS:
        peers = peers + inside(off, 1).astype(jnp.int32)
    pl.semaphore_wait(barrier, peers)

    def copy(which, direction):
        off, sign = OFFSETS[direction], signs[which]
        return pltpu.make_async_remote_copy(
            src_ref=sources[which].at[direction],
            dst_ref=targets[which].at[direction],
            send_sem=send_sem.at[which, direction],
            recv_sem=recv_sem.at[which, direction],
            device_id=(here_x + sign * off[0], here_y + sign * off[1]),
            device_id_type=MESH,
        )

    pairs = [(which, d) for which in range(count) for d in range(len(OFFSETS))]
    for which, d in pairs:

        @pl.when(inside(OFFSETS[d], signs[which]))
        def _():
            copy(which, d).start()

    for which, d in pairs:

        @pl.when(inside(OFFSETS[d], -signs[which]))
        def _():
            copy(which, d).wait_recv()

    for which, d in pairs:

        @pl.when(inside(OFFSETS[d], signs[which]))
        def _():
            copy(which, d).wait_send()


def sum_kernel(n_gx, n_gy, partial, total, slots_y, slots_x, middle, send_y, recv_y, send_x, recv_x):
    here_x, here_y = lax.axis_index("gx"), lax.axis_index("gy")
    barrier = pltpu.get_barrier_semaphore()
    for r in range(1, n_gy):
        pl.semaphore_signal(
            barrier, inc=1, device_id=(here_x, lax.rem(here_y + r, n_gy)), device_id_type=MESH
        )
    for r in range(1, n_gx):
        pl.semaphore_signal(
            barrier, inc=1, device_id=(lax.rem(here_x + r, n_gx), here_y), device_id_type=MESH
        )
    pl.semaphore_wait(barrier, n_gx + n_gy - 2)

    def phase(source, slots, size, here, device, send_sem, recv_sem):
        copies = []
        for r in range(1, size):
            copies.append(
                pltpu.make_async_remote_copy(
                    src_ref=source,
                    dst_ref=slots.at[here],
                    send_sem=send_sem.at[r],
                    recv_sem=recv_sem.at[r],
                    device_id=device(lax.rem(here + r, size)),
                    device_id_type=MESH,
                )
            )
            copies[-1].start()
        slots[here] = source[...]
        for item in copies:
            item.wait()
        result = slots[0]
        for s in range(1, size):
            result = result + slots[s]
        return result

    middle[...] = phase(partial, slots_y, n_gy, here_y, lambda t: (here_x, t), send_y, recv_y)
    total[...] = phase(middle, slots_x, n_gx, here_x, lambda t: (t, here_y), send_x, recv_x)


def local(
    n_gx, n_gy,
    vol_rhs, trace_in, pml_flag, stretch, cond_op, skel_op, block_coef, recon_op, lift_op,
    elem_face, adjacency, halo_list,
):
    f32 = jnp.float32
    faces = trace_in.shape[2]
    elems = vol_rhs.shape[2]
    half = trace_in.shape[1]
    rows = 2 * half
    neighbours = adjacency.shape[0]
    dirs, halo_len = halo_list.shape
    halo = dirs * halo_len
    shape = jax.ShapeDtypeStruct

    slot = elem_face.reshape(-1)
    flat_lists = halo_list.reshape(-1)
    lists = jnp.maximum(flat_lists, 0)
    owners = jnp.where(flat_lists >= 0, flat_lists, faces)
    adjacent = jnp.maximum(adjacency, 0).reshape(-1)
    live = jnp.concatenate([jnp.ones((1, faces), bool), adjacency >= 0], axis=0)
    coef = jnp.where(live[:, None], block_coef, 0.0).reshape(2 * (neighbours + 1), faces)
    coef = jnp.pad(coef.T, ((0, 0), (0, 16 - coef.shape[0])))

    blocks = jax.vmap(complex_block)(skel_op).transpose(0, 2, 1)
    weights = jnp.concatenate([pad_lanes(blocks), pad_lanes(times_i(blocks))], axis=-1)
    weights = jnp.pad(weights, ((0, 0), (0, LANES - rows), (0, 0)))
    high = lax.reduce_precision(weights, 8, 7)
    high, low = high.astype(jnp.bfloat16), (weights - high).astype(jnp.bfloat16)
    weights = jnp.stack([jnp.concatenate([w, w], axis=1) for w in (high, low)], axis=1)

    own = pad_lanes(trace_in.reshape(rows, faces).T)
    volume = vol_rhs.reshape(2 * vol_rhs.shape[1], elems)
    tilt = pml_flag.astype(f32) * stretch
    cond = jax.vmap(complex_block)(cond_op)
    cond = pad_lanes(cond.transpose(0, 2, 1))
    cond_i = pad_lanes(times_i(jax.vmap(complex_block)(cond_op).transpose(0, 2, 1)))

    def condense(matrix):
        return jnp.einsum(
            "ke,ikc->iec", volume, matrix, precision=lax.Precision.HIGHEST, preferred_element_type=f32
        )

    pieces = condense(cond) + tilt[None, :, None] * condense(cond_i)
    pieces = pieces.reshape(4 * elems, LANES)

    params = pltpu.CompilerParams(vmem_limit_bytes=BIG)
    table = pltpu.VMEM((faces + halo, LANES), f32)
    collected, parcels = pl.pallas_call(
        scatter_kernel,
        out_shape=(shape((faces + halo, LANES), f32), shape((halo, LANES), f32)),
        in_specs=[SMEM, SMEM, VMEM, VMEM],
        out_specs=(VMEM, VMEM),
        scratch_shapes=[table] * 3,
        compiler_params=params,
    )(slot, lists, pieces, own)

    def exchange(arrays, signs, number):
        blocked = [a.reshape(dirs, halo_len, LANES) for a in arrays]
        result = pl.pallas_call(
            functools.partial(exchange_kernel, signs, n_gx, n_gy),
            out_shape=tuple(shape((dirs, halo_len, LANES), f32) for _ in arrays),
            in_specs=[VMEM] * len(arrays),
            out_specs=(VMEM,) * len(arrays),
            scratch_shapes=[pltpu.SemaphoreType.DMA((len(arrays), dirs))] * 2,
            compiler_params=pltpu.CompilerParams(collective_id=number, has_side_effects=True),
        )(*blocked)
        return [r.reshape(halo, LANES) for r in result]

    returned, ghost = exchange([collected[faces:], parcels], (-1, 1), 0)

    gathered = pltpu.VMEM((neighbours, TILE, LANES), f32)
    residual, parcels = pl.pallas_call(
        residual_kernel,
        out_shape=(shape((faces, LANES), f32), shape((halo, LANES), f32)),
        in_specs=[SMEM] * 3 + [VMEM] * 6,
        out_specs=(VMEM, VMEM),
        scratch_shapes=[table, gathered, pltpu.VMEM((faces + 8, LANES), f32)],
        compiler_params=params,
    )(adjacent, lists, owners, coef, weights, own, ghost, collected[:faces], returned)

    (ghost_residual,) = exchange([parcels], (1,), 1)

    picked_trace = pl.pallas_call(
        pick_kernel,
        out_shape=shape((4 * elems, LANES), f32),
        in_specs=[SMEM] + [VMEM] * 2,
        out_specs=VMEM,
        scratch_shapes=[table],
        compiler_params=params,
    )(slot, own, ghost)

    partial, picked_residual = pl.pallas_call(
        functools.partial(image_kernel, half),
        out_shape=(shape((8, LANES), f32), shape((4 * elems, LANES), f32)),
        in_specs=[SMEM] * 2 + [VMEM] * 4,
        out_specs=(VMEM, VMEM),
        scratch_shapes=[table, gathered],
        compiler_params=params,
    )(adjacent, slot, coef, weights, residual, ghost_residual)

    tile = (8, LANES)
    total = pl.pallas_call(
        functools.partial(sum_kernel, n_gx, n_gy),
        out_shape=shape(tile, f32),
        in_specs=[VMEM],
        out_specs=VMEM,
        scratch_shapes=[
            pltpu.VMEM((n_gy,) + tile, f32),
            pltpu.VMEM((n_gx,) + tile, f32),
            pltpu.VMEM(tile, f32),
            pltpu.SemaphoreType.DMA((n_gy,)),
            pltpu.SemaphoreType.DMA((n_gy,)),
            pltpu.SemaphoreType.DMA((n_gx,)),
            pltpu.SemaphoreType.DMA((n_gx,)),
        ],
        compiler_params=pltpu.CompilerParams(collective_id=2, has_side_effects=True),
    )(partial)
    sums = jnp.sum(total, axis=1)
    step_real = sums[0] / sums[2]
    step_imag = sums[1] / sums[2]

    change = residual[:, :rows].T.reshape(2, half, faces)
    trace_out = trace_in + jnp.stack(
        [step_real * change[0] - step_imag * change[1], step_real * change[1] + step_imag * change[0]]
    )

    lift = jax.vmap(complex_block)(lift_op).transpose(0, 2, 1)
    lift_i = times_i(lift)
    lift_rows = jnp.pad(lift, ((0, 0), (0, LANES - rows), (0, 0)))
    lift_rows_i = jnp.pad(lift_i, ((0, 0), (0, LANES - rows), (0, 0)))

    def lifted(matrix, picked):
        return jnp.einsum(
            "icv,iec->ve", matrix, picked.reshape(4, elems, LANES),
            precision=lax.Precision.HIGHEST, preferred_element_type=f32,
        )

    stepped = step_real * lift_rows + step_imag * lift_rows_i
    base = jnp.dot(
        complex_block(recon_op), volume, precision=lax.Precision.HIGHEST, preferred_element_type=f32
    )
    mid = base.shape[0] // 2
    base = jnp.concatenate(
        [base[:mid] - tilt * base[mid:], base[mid:] + tilt * base[:mid]], axis=0
    )
    volume_out = base - lifted(lift_rows, picked_trace) - lifted(stepped, picked_residual)
    return trace_out, volume_out.reshape(vol_rhs.shape)


def solution(mesh):
    split_last = P(None, None, ("gx", "gy"))
    in_specs = (
        split_last, split_last, P(("gx", "gy")), P(("gx", "gy")), P(), P(), split_last, P(), P(),
        P(None, ("gx", "gy")), P(None, ("gx", "gy")), P(None, ("gx", "gy")),
    )
    return jax.shard_map(
        functools.partial(local, mesh.shape["gx"], mesh.shape["gy"]),
        mesh=mesh,
        in_specs=in_specs,
        out_specs=(split_last, split_last),
        check_vma=False,
    )
```

```python
import functools

import jax
import jax.numpy as jnp
from jax import lax
from jax.experimental import pallas as pl
from jax.experimental.pallas import tpu as pltpu
from jax.sharding import PartitionSpec as P

OFFSETS = ((-1, -1), (-1, 0), (-1, 1), (0, -1), (0, 1), (1, -1), (1, 0), (1, 1))
LANES = 128
TILE = 256
MESH = pl.DeviceIdType.MESH
VMEM = pl.BlockSpec(memory_space=pltpu.VMEM)
SMEM = pl.BlockSpec(memory_space=pltpu.SMEM)
BIG = 60 * 1024 * 1024


def complex_block(complex_pair):
    top_row = jnp.concatenate([complex_pair[0], -complex_pair[1]], axis=1)
    bottom_row = jnp.concatenate([complex_pair[1], complex_pair[0]], axis=1)
    return jnp.concatenate([top_row, bottom_row], axis=0)


def times_i(rows):
    half = rows.shape[-1] // 2
    return jnp.concatenate([-rows[..., half:], rows[..., :half]], axis=-1)


def pad_lanes(rows):
    return jnp.pad(rows, ((0, 0),) * (rows.ndim - 1) + ((0, LANES - rows.shape[-1]),))


def split(x):
    high = x.astype(jnp.bfloat16)
    return high, (x - high.astype(jnp.float32)).astype(jnp.bfloat16)


def gather_rows(source, index, index_base, target, count, group=32):
    @pl.loop(0, count // group)
    def _(step):
        base = step * group
        rows = [source[pl.ds(index[index_base + base + u], 1), :] for u in range(group)]
        for u in range(group):
            target[pl.ds(index_base + base + u, 1), :] = rows[u]


def pack(rows, width, target):
    half, extra = LANES // 2, width - LANES // 2
    count = rows.shape[0]
    mid, groups = count // 2, LANES // extra
    lane = lax.broadcasted_iota(jnp.int32, (mid, LANES), 1)
    target[:mid, :] = jnp.where(lane < half, rows[:mid], pltpu.roll(rows[mid:], half, 1))
    piece = count // groups
    small_lane = lax.broadcasted_iota(jnp.int32, (piece, LANES), 1)
    tail = jnp.zeros((piece, LANES), jnp.float32)
    for g in range(groups):
        part = rows[g * piece : (g + 1) * piece]
        shift = (g * extra - half) % LANES
        part = pltpu.roll(part, shift, 1) if shift else part
        tail = jnp.where((small_lane >= g * extra) & (small_lane < (g + 1) * extra), part, tail)
    target[mid:, :] = tail


def unpack(packed, width, count):
    half, extra = LANES // 2, width - LANES // 2
    mid, groups = count // 2, LANES // extra
    piece = count // groups
    front, tail = packed[:mid], packed[mid:]
    parts = []
    for g in range(groups):
        shift = (half - g * extra) % LANES
        parts.append(pltpu.roll(tail, shift, 1) if shift else tail)
    ends = jnp.concatenate(parts, axis=0)
    starts = jnp.concatenate([front, pltpu.roll(front, half, 1)], axis=0)
    lane = lax.broadcasted_iota(jnp.int32, (count, LANES), 1)
    return jnp.where(lane < half, starts, jnp.where(lane < width, ends, 0.0))


def pack_all(source, first, halo_len, width, target):
    @pl.loop(0, target.shape[0])
    def _(d):
        base = pl.multiple_of(first + d * halo_len, 8)
        pack(source[pl.ds(base, halo_len), :], width, target.at[d])


def unpack_all(source, width, target, first, halo_len):
    @pl.loop(0, source.shape[0])
    def _(d):
        base = pl.multiple_of(first + d * halo_len, 8)
        target[pl.ds(base, halo_len), :] = unpack(source[d], width, halo_len)


def scatter_kernel(
    width, slot, lists, pieces, own, collected, packed_trace, packed_sums, total, part1, part2, part3
):
    count = pieces.shape[0] // 4
    faces = own.shape[0]
    halo_len = lists.shape[0] // packed_trace.shape[0]
    gather_rows(own, lists, 0, total, lists.shape[0])
    pack_all(total, 0, halo_len, width, packed_trace)
    parts = (total, part1, part2, part3)
    for part in parts:
        part[...] = jnp.zeros_like(part)

    @pl.loop(0, count // 8)
    def _(step):
        for u in range(8):
            e = step * 8 + u
            places = [slot[corner * count + e] for corner in range(4)]
            sums = [
                parts[corner][pl.ds(places[corner], 1), :] + pieces[pl.ds(corner * count + e, 1), :]
                for corner in range(4)
            ]
            for corner in range(4):
                parts[corner][pl.ds(places[corner], 1), :] = sums[corner]

    def joined(rows):
        return (total[rows, :] + part1[rows, :]) + (part2[rows, :] + part3[rows, :])

    @pl.loop(0, faces // TILE)
    def _(step):
        rows = pl.ds(pl.multiple_of(step * TILE, TILE), TILE)
        collected[rows, :] = joined(rows)

    @pl.loop(0, packed_sums.shape[0])
    def _(d):
        rows = pl.ds(pl.multiple_of(faces + d * halo_len, 8), halo_len)
        pack(joined(rows), width, packed_sums.at[d])


def apply_skeleton(adjacent, extended, coef, weights, gathered, finish):
    faces = coef.shape[0]
    neighbours = gathered.shape[0]

    @pl.loop(0, faces // TILE)
    def _(step):
        base = pl.multiple_of(step * TILE, TILE)

        @pl.loop(0, TILE // 8)
        def _(group):
            first = group * 8
            for k in range(neighbours):
                rows = [
                    extended[pl.ds(adjacent[k * faces + base + first + u], 1), :] for u in range(8)
                ]
                for u in range(8):
                    gathered[k, pl.ds(first + u, 1), :] = rows[u]

        scale = coef[pl.ds(base, TILE), :]
        total = None
        for k in range(neighbours + 1):
            x = extended[pl.ds(base, TILE), :] if k == 0 else gathered[k - 1]
            both = jnp.concatenate(split(x), axis=1)
            y = jnp.dot(both, weights[k, 0], preferred_element_type=jnp.float32)
            y += jnp.dot(both, weights[k, 1], preferred_element_type=jnp.float32)
            term = scale[:, 2 * k : 2 * k + 1] * y[:, :LANES] + scale[:, 2 * k + 1 : 2 * k + 2] * y[:, LANES:]
            total = term if total is None else total + term
        finish(base, total)


def inside(n_gx, n_gy, off, sign):
    x, y = lax.axis_index("gx") + sign * off[0], lax.axis_index("gy") + sign * off[1]
    return (x >= 0) & (x < n_gx) & (y >= 0) & (y < n_gy)


def greet(n_gx, n_gy, lines):
    here_x, here_y = lax.axis_index("gx"), lax.axis_index("gy")
    barrier = pltpu.get_barrier_semaphore()
    peers = 0
    for off in OFFSETS:

        @pl.when(inside(n_gx, n_gy, off, 1))
        def _():
            pl.semaphore_signal(
                barrier, inc=1, device_id=(here_x + off[0], here_y + off[1]), device_id_type=MESH
            )

        peers = peers + inside(n_gx, n_gy, off, 1).astype(jnp.int32)
    if lines:
        for r in range(1, n_gy):
            pl.semaphore_signal(
                barrier, inc=1, device_id=(here_x, lax.rem(here_y + r, n_gy)), device_id_type=MESH
            )
        for r in range(1, n_gx):
            pl.semaphore_signal(
                barrier, inc=1, device_id=(lax.rem(here_x + r, n_gx), here_y), device_id_type=MESH
            )
        peers = peers + (n_gx + n_gy - 2)
    pl.semaphore_wait(barrier, peers)


class Exchange:
    def __init__(self, n_gx, n_gy, sign, source, target, send_sem, recv_sem):
        self.grid, self.sign = (n_gx, n_gy), sign
        self.refs = source, target, send_sem, recv_sem

    def copy(self, d):
        source, target, send_sem, recv_sem = self.refs
        off, sign = OFFSETS[d], self.sign
        return pltpu.make_async_remote_copy(
            src_ref=source.at[d],
            dst_ref=target.at[d],
            send_sem=send_sem.at[d],
            recv_sem=recv_sem.at[d],
            device_id=(lax.axis_index("gx") + sign * off[0], lax.axis_index("gy") + sign * off[1]),
            device_id_type=MESH,
        )

    def each(self, sign, act):
        for d in range(len(OFFSETS)):

            @pl.when(inside(*self.grid, OFFSETS[d], sign))
            def _():
                act(self.copy(d))

    def start(self):
        self.each(self.sign, lambda copy: copy.start())

    def receive(self):
        self.each(-self.sign, lambda copy: copy.wait_recv())

    def finish(self):
        self.each(self.sign, lambda copy: copy.wait_send())


def trace_kernel(
    n_gx, n_gy, width, adjacent, coef, weights, own, packed_trace, packed_sums,
    applied, extended, returned, arrived, gathered, send_a, recv_a, send_b, recv_b,
):
    faces = own.shape[0]
    halo_len = (extended.shape[0] - faces) // packed_trace.shape[0]
    greet(n_gx, n_gy, False)
    first = Exchange(n_gx, n_gy, 1, packed_trace, arrived, send_a, recv_a)
    second = Exchange(n_gx, n_gy, -1, packed_sums, returned, send_b, recv_b)
    first.start()
    extended[:faces, :] = own[...]
    first.receive()
    second.start()
    unpack_all(arrived, width, extended, faces, halo_len)

    def finish(base, total):
        applied[pl.ds(base, TILE), :] = total

    apply_skeleton(adjacent, extended, coef, weights, gathered, finish)
    second.receive()
    first.finish()
    second.finish()


def residual_kernel(
    width, lists, owners, applied, collected, returned, residual, packed, sums, rows_back
):
    faces = applied.shape[0]
    halo_len = lists.shape[0] // packed.shape[0]
    sums[:faces, :] = collected[...] - applied[...]
    unpack_all(returned, width, rows_back, 0, halo_len)

    @pl.loop(0, lists.shape[0] // 16)
    def _(step):
        places = [owners[step * 16 + u] for u in range(16)]
        rows = [
            sums[pl.ds(places[u], 1), :] + rows_back[pl.ds(step * 16 + u, 1), :] for u in range(16)
        ]
        for u in range(16):
            sums[pl.ds(places[u], 1), :] = rows[u]

    residual[...] = sums[:faces, :]
    gather_rows(sums, lists, 0, rows_back, lists.shape[0])
    pack_all(rows_back, 0, halo_len, width, packed)


def line_copies(source, slots, size, here, device, send_sem, recv_sem):
    copies = []
    for r in range(1, size):
        copies.append(
            pltpu.make_async_remote_copy(
                src_ref=source,
                dst_ref=slots.at[here],
                send_sem=send_sem.at[r],
                recv_sem=recv_sem.at[r],
                device_id=device(lax.rem(here + r, size)),
                device_id_type=MESH,
            )
        )
        copies[-1].start()
    slots[here] = source[...]
    return copies


def line_sum(copies, slots, size):
    for item in copies:
        item.wait()
    result = slots[0]
    for s in range(1, size):
        result = result + slots[s]
    return result


def image_kernel(
    n_gx, n_gy, width, adjacent, slot, coef, weights, own, table, packed,
    total_out, picked_trace, picked_residual,
    arrived, extended, gathered, partial, middle, slots_y, slots_x,
    send_a, recv_a, send_y, recv_y, send_x, recv_x,
):
    faces = own.shape[0]
    half = width // 2
    halo_len = (extended.shape[0] - faces) // packed.shape[0]
    here_x, here_y = lax.axis_index("gx"), lax.axis_index("gy")
    greet(n_gx, n_gy, True)
    halo = Exchange(n_gx, n_gy, 1, packed, arrived, send_a, recv_a)
    halo.start()
    extended[:faces, :] = own[...]
    partial[...] = jnp.zeros_like(partial)
    count = picked_trace.shape[0]
    gather_rows(table, slot, 0, picked_trace, count)
    halo.receive()
    unpack_all(arrived, width, extended, faces, halo_len)
    lane = lax.broadcasted_iota(jnp.int32, (TILE, LANES), 1)

    def finish(base, total):
        res = extended[pl.ds(base, TILE), :]
        down = pltpu.roll(res, LANES - half, 1)
        up = pltpu.roll(res, half, 1)
        turned = jnp.where(lane < half, down, -up)
        partial[0:1, :] += jnp.sum(total * res, axis=0, keepdims=True)
        partial[1:2, :] += jnp.sum(total * turned, axis=0, keepdims=True)
        partial[2:3, :] += jnp.sum(total * total, axis=0, keepdims=True)

    apply_skeleton(adjacent, extended, coef, weights, gathered, finish)
    copies = line_copies(partial, slots_y, n_gy, here_y, lambda t: (here_x, t), send_y, recv_y)
    gather_rows(extended, slot, 0, picked_residual, count // 2)
    middle[...] = line_sum(copies, slots_y, n_gy)
    copies = line_copies(middle, slots_x, n_gx, here_x, lambda t: (t, here_y), send_x, recv_x)
    gather_rows(extended, slot, count // 2, picked_residual, count // 2)
    total_out[...] = line_sum(copies, slots_x, n_gx)
    halo.finish()


def local(
    n_gx, n_gy,
    vol_rhs, trace_in, pml_flag, stretch, cond_op, skel_op, block_coef, recon_op, lift_op,
    elem_face, adjacency, halo_list,
):
    f32 = jnp.float32
    faces = trace_in.shape[2]
    elems = vol_rhs.shape[2]
    half = trace_in.shape[1]
    rows = 2 * half
    neighbours = adjacency.shape[0]
    dirs, halo_len = halo_list.shape
    halo = dirs * halo_len
    shape = jax.ShapeDtypeStruct

    slot = elem_face.reshape(-1)
    flat_lists = halo_list.reshape(-1)
    lists = jnp.maximum(flat_lists, 0)
    owners = jnp.where(flat_lists >= 0, flat_lists, faces)
    adjacent = jnp.maximum(adjacency, 0).reshape(-1)
    live = jnp.concatenate([jnp.ones((1, faces), bool), adjacency >= 0], axis=0)
    coef = jnp.where(live[:, None], block_coef, 0.0).reshape(2 * (neighbours + 1), faces)
    coef = jnp.pad(coef.T, ((0, 0), (0, 16 - coef.shape[0])))

    blocks = jax.vmap(complex_block)(skel_op).transpose(0, 2, 1)
    weights = jnp.concatenate([pad_lanes(blocks), pad_lanes(times_i(blocks))], axis=-1)
    weights = jnp.pad(weights, ((0, 0), (0, LANES - rows), (0, 0)))
    high = lax.reduce_precision(weights, 8, 7)
    high, low = high.astype(jnp.bfloat16), (weights - high).astype(jnp.bfloat16)
    weights = jnp.stack([jnp.concatenate([w, w], axis=1) for w in (high, low)], axis=1)

    own = pad_lanes(trace_in.reshape(rows, faces).T)
    volume = vol_rhs.reshape(2 * vol_rhs.shape[1], elems)
    tilt = pml_flag.astype(f32) * stretch
    cond = jax.vmap(complex_block)(cond_op)
    cond = pad_lanes(cond.transpose(0, 2, 1))
    cond_i = pad_lanes(times_i(jax.vmap(complex_block)(cond_op).transpose(0, 2, 1)))

    def condense(matrix):
        return jnp.einsum(
            "ke,ikc->iec", volume, matrix, precision=lax.Precision.HIGHEST, preferred_element_type=f32
        )

    pieces = condense(cond) + tilt[None, :, None] * condense(cond_i)
    pieces = pieces.reshape(4 * elems, LANES)

    params = pltpu.CompilerParams(vmem_limit_bytes=BIG)
    table = pltpu.VMEM((faces + halo, LANES), f32)
    rows_shape = shape((faces, LANES), f32)
    packed_dims = (dirs, halo_len * rows // LANES, LANES)
    packed_shape = shape(packed_dims, f32)
    collected, packed_trace, packed_sums = pl.pallas_call(
        functools.partial(scatter_kernel, rows),
        out_shape=(rows_shape, packed_shape, packed_shape),
        in_specs=[SMEM, SMEM, VMEM, VMEM],
        out_specs=(VMEM,) * 3,
        scratch_shapes=[table] * 4,
        compiler_params=params,
    )(slot, lists, pieces, own)

    def talking(number):
        return pltpu.CompilerParams(
            collective_id=number, has_side_effects=True, vmem_limit_bytes=BIG
        )

    halo_sem = pltpu.SemaphoreType.DMA((dirs,))
    gathered = pltpu.VMEM((neighbours, TILE, LANES), f32)
    applied, extended, returned = pl.pallas_call(
        functools.partial(trace_kernel, n_gx, n_gy, rows),
        out_shape=(rows_shape, shape((faces + halo, LANES), f32), packed_shape),
        in_specs=[SMEM] + [VMEM] * 5,
        out_specs=(VMEM,) * 3,
        scratch_shapes=[pltpu.VMEM(packed_dims, f32), gathered] + [halo_sem] * 4,
        compiler_params=talking(0),
    )(adjacent, coef, weights, own, packed_trace, packed_sums)

    residual, packed = pl.pallas_call(
        functools.partial(residual_kernel, rows),
        out_shape=(rows_shape, packed_shape),
        in_specs=[SMEM] * 2 + [VMEM] * 3,
        out_specs=(VMEM, VMEM),
        scratch_shapes=[pltpu.VMEM((faces + 8, LANES), f32), pltpu.VMEM((halo, LANES), f32)],
        compiler_params=params,
    )(lists, owners, applied, collected, returned)

    tile = (8, LANES)
    picked_shape = shape((4 * elems, LANES), f32)
    total, picked_trace, picked_residual = pl.pallas_call(
        functools.partial(image_kernel, n_gx, n_gy, rows),
        out_shape=(shape(tile, f32), picked_shape, picked_shape),
        in_specs=[SMEM] * 2 + [VMEM] * 5,
        out_specs=(VMEM,) * 3,
        scratch_shapes=[
            pltpu.VMEM(packed_dims, f32), table, gathered,
            pltpu.VMEM(tile, f32), pltpu.VMEM(tile, f32),
            pltpu.VMEM((n_gy,) + tile, f32), pltpu.VMEM((n_gx,) + tile, f32),
        ]
        + [halo_sem] * 2
        + [pltpu.SemaphoreType.DMA((n_gy,))] * 2
        + [pltpu.SemaphoreType.DMA((n_gx,))] * 2,
        compiler_params=talking(1),
    )(adjacent, slot, coef, weights, residual, extended, packed)
    sums = jnp.sum(total, axis=1)
    step_real = sums[0] / sums[2]
    step_imag = sums[1] / sums[2]

    change = residual[:, :rows].T.reshape(2, half, faces)
    trace_out = trace_in + jnp.stack(
        [step_real * change[0] - step_imag * change[1], step_real * change[1] + step_imag * change[0]]
    )

    lift = jax.vmap(complex_block)(lift_op).transpose(0, 2, 1)
    lift_i = times_i(lift)
    lift_rows = jnp.pad(lift, ((0, 0), (0, LANES - rows), (0, 0)))
    lift_rows_i = jnp.pad(lift_i, ((0, 0), (0, LANES - rows), (0, 0)))

    def lifted(matrix, picked):
        return jnp.einsum(
            "icv,iec->ve", matrix, picked.reshape(4, elems, LANES),
            precision=lax.Precision.HIGHEST, preferred_element_type=f32,
        )

    stepped = step_real * lift_rows + step_imag * lift_rows_i
    base = jnp.dot(
        complex_block(recon_op), volume, precision=lax.Precision.HIGHEST, preferred_element_type=f32
    )
    mid = base.shape[0] // 2
    base = jnp.concatenate(
        [base[:mid] - tilt * base[mid:], base[mid:] + tilt * base[:mid]], axis=0
    )
    volume_out = base - lifted(lift_rows, picked_trace) - lifted(stepped, picked_residual)
    return trace_out, volume_out.reshape(vol_rhs.shape)


def solution(mesh):
    split_last = P(None, None, ("gx", "gy"))
    in_specs = (
        split_last, split_last, P(("gx", "gy")), P(("gx", "gy")), P(), P(), split_last, P(), P(),
        P(None, ("gx", "gy")), P(None, ("gx", "gy")), P(None, ("gx", "gy")),
    )
    return jax.shard_map(
        functools.partial(local, mesh.shape["gx"], mesh.shape["gy"]),
        mesh=mesh,
        in_specs=in_specs,
        out_specs=(split_last, split_last),
        check_vma=False,
    )
```

```python
import functools

import jax
import jax.numpy as jnp
from jax import lax
from jax.experimental import pallas as pl
from jax.experimental.pallas import tpu as pltpu
from jax.sharding import PartitionSpec as P

OFFSETS = ((-1, -1), (-1, 0), (-1, 1), (0, -1), (0, 1), (1, -1), (1, 0), (1, 1))
LANES = 128
TILE = 256
MESH = pl.DeviceIdType.MESH
VMEM = pl.BlockSpec(memory_space=pltpu.VMEM)
SMEM = pl.BlockSpec(memory_space=pltpu.SMEM)
BIG = 60 * 1024 * 1024


def complex_block(complex_pair):
    top_row = jnp.concatenate([complex_pair[0], -complex_pair[1]], axis=1)
    bottom_row = jnp.concatenate([complex_pair[1], complex_pair[0]], axis=1)
    return jnp.concatenate([top_row, bottom_row], axis=0)


def times_i(rows):
    half = rows.shape[-1] // 2
    return jnp.concatenate([-rows[..., half:], rows[..., :half]], axis=-1)


def pad_lanes(rows):
    return jnp.pad(rows, ((0, 0),) * (rows.ndim - 1) + ((0, LANES - rows.shape[-1]),))


def split(x):
    high = x.astype(jnp.bfloat16)
    return high, (x - high.astype(jnp.float32)).astype(jnp.bfloat16)


def gather_rows(source, index, index_base, target, count, group=32):
    @pl.loop(0, count // group)
    def _(step):
        base = step * group
        views = [index.at[pl.ds(index_base + base + first, 8)] for first in range(0, group, 8)]
        rows = [source[pl.ds(views[u // 8][u % 8], 1), :] for u in range(group)]
        for u in range(group):
            target[pl.ds(index_base + base + u, 1), :] = rows[u]


def pack(rows, width, target):
    half, extra = LANES // 2, width - LANES // 2
    count = rows.shape[0]
    mid, groups = count // 2, LANES // extra
    lane = lax.broadcasted_iota(jnp.int32, (mid, LANES), 1)
    target[:mid, :] = jnp.where(lane < half, rows[:mid], pltpu.roll(rows[mid:], half, 1))
    piece = count // groups
    small_lane = lax.broadcasted_iota(jnp.int32, (piece, LANES), 1)
    tail = jnp.zeros((piece, LANES), jnp.float32)
    for g in range(groups):
        part = rows[g * piece : (g + 1) * piece]
        shift = (g * extra - half) % LANES
        part = pltpu.roll(part, shift, 1) if shift else part
        tail = jnp.where((small_lane >= g * extra) & (small_lane < (g + 1) * extra), part, tail)
    target[mid:, :] = tail


def unpack(packed, width, count):
    half, extra = LANES // 2, width - LANES // 2
    mid, groups = count // 2, LANES // extra
    piece = count // groups
    front, tail = packed[:mid], packed[mid:]
    parts = []
    for g in range(groups):
        shift = (half - g * extra) % LANES
        parts.append(pltpu.roll(tail, shift, 1) if shift else tail)
    ends = jnp.concatenate(parts, axis=0)
    starts = jnp.concatenate([front, pltpu.roll(front, half, 1)], axis=0)
    lane = lax.broadcasted_iota(jnp.int32, (count, LANES), 1)
    return jnp.where(lane < half, starts, jnp.where(lane < width, ends, 0.0))


def pack_all(source, first, halo_len, width, target):
    @pl.loop(0, target.shape[0])
    def _(d):
        base = pl.multiple_of(first + d * halo_len, 8)
        pack(source[pl.ds(base, halo_len), :], width, target.at[d])


def unpack_all(source, width, target, first, halo_len):
    @pl.loop(0, source.shape[0])
    def _(d):
        base = pl.multiple_of(first + d * halo_len, 8)
        target[pl.ds(base, halo_len), :] = unpack(source[d], width, halo_len)


def scatter_kernel(
    width, slot, lists, pieces, own, collected, packed_trace, packed_sums, total, part1, part2, part3
):
    count = pieces.shape[0] // 4
    faces = own.shape[0]
    halo_len = lists.shape[0] // packed_trace.shape[0]
    gather_rows(own, lists, 0, total, lists.shape[0])
    pack_all(total, 0, halo_len, width, packed_trace)
    parts = (total, part1, part2, part3)
    for part in parts:
        part[...] = jnp.zeros_like(part)

    @pl.loop(0, count // 8)
    def _(step):
        for u in range(8):
            e = step * 8 + u
            places = [slot[corner * count + e] for corner in range(4)]
            sums = [
                parts[corner][pl.ds(places[corner], 1), :] + pieces[pl.ds(corner * count + e, 1), :]
                for corner in range(4)
            ]
            for corner in range(4):
                parts[corner][pl.ds(places[corner], 1), :] = sums[corner]

    def joined(rows):
        return (total[rows, :] + part1[rows, :]) + (part2[rows, :] + part3[rows, :])

    @pl.loop(0, faces // TILE)
    def _(step):
        rows = pl.ds(pl.multiple_of(step * TILE, TILE), TILE)
        collected[rows, :] = joined(rows)

    @pl.loop(0, packed_sums.shape[0])
    def _(d):
        rows = pl.ds(pl.multiple_of(faces + d * halo_len, 8), halo_len)
        pack(joined(rows), width, packed_sums.at[d])


def apply_skeleton(adjacent, extended, coef, weights, gathered, finish):
    faces = coef.shape[0]
    neighbours = gathered.shape[0]

    @pl.loop(0, faces // TILE)
    def _(step):
        base = pl.multiple_of(step * TILE, TILE)

        @pl.loop(0, TILE // 8)
        def _(group):
            first = group * 8
            for k in range(neighbours):
                view = adjacent.at[pl.ds(k * faces + base + first, 8)]
                rows = [extended[pl.ds(view[u], 1), :] for u in range(8)]
                for u in range(8):
                    gathered[k, pl.ds(first + u, 1), :] = rows[u]

        scale = coef[pl.ds(base, TILE), :]
        total = None
        for k in range(neighbours + 1):
            x = extended[pl.ds(base, TILE), :] if k == 0 else gathered[k - 1]
            both = jnp.concatenate(split(x), axis=1)
            y = jnp.dot(both, weights[k, 0], preferred_element_type=jnp.float32)
            y += jnp.dot(both, weights[k, 1], preferred_element_type=jnp.float32)
            term = scale[:, 2 * k : 2 * k + 1] * y[:, :LANES] + scale[:, 2 * k + 1 : 2 * k + 2] * y[:, LANES:]
            total = term if total is None else total + term
        finish(base, total)


def inside(n_gx, n_gy, off, sign):
    x, y = lax.axis_index("gx") + sign * off[0], lax.axis_index("gy") + sign * off[1]
    return (x >= 0) & (x < n_gx) & (y >= 0) & (y < n_gy)


def greet(n_gx, n_gy, lines):
    here_x, here_y = lax.axis_index("gx"), lax.axis_index("gy")
    barrier = pltpu.get_barrier_semaphore()
    peers = 0
    for off in OFFSETS:

        @pl.when(inside(n_gx, n_gy, off, 1))
        def _():
            pl.semaphore_signal(
                barrier, inc=1, device_id=(here_x + off[0], here_y + off[1]), device_id_type=MESH
            )

        peers = peers + inside(n_gx, n_gy, off, 1).astype(jnp.int32)
    if lines:
        for r in range(1, n_gy):
            pl.semaphore_signal(
                barrier, inc=1, device_id=(here_x, lax.rem(here_y + r, n_gy)), device_id_type=MESH
            )
        for r in range(1, n_gx):
            pl.semaphore_signal(
                barrier, inc=1, device_id=(lax.rem(here_x + r, n_gx), here_y), device_id_type=MESH
            )
        peers = peers + (n_gx + n_gy - 2)
    pl.semaphore_wait(barrier, peers)


class Exchange:
    def __init__(self, n_gx, n_gy, sign, source, target, send_sem, recv_sem):
        self.grid, self.sign = (n_gx, n_gy), sign
        self.refs = source, target, send_sem, recv_sem

    def copy(self, d):
        source, target, send_sem, recv_sem = self.refs
        off, sign = OFFSETS[d], self.sign
        return pltpu.make_async_remote_copy(
            src_ref=source.at[d],
            dst_ref=target.at[d],
            send_sem=send_sem.at[d],
            recv_sem=recv_sem.at[d],
            device_id=(lax.axis_index("gx") + sign * off[0], lax.axis_index("gy") + sign * off[1]),
            device_id_type=MESH,
        )

    def each(self, sign, act):
        for d in range(len(OFFSETS)):

            @pl.when(inside(*self.grid, OFFSETS[d], sign))
            def _():
                act(self.copy(d))

    def start(self):
        self.each(self.sign, lambda copy: copy.start())

    def receive(self):
        self.each(-self.sign, lambda copy: copy.wait_recv())

    def finish(self):
        self.each(self.sign, lambda copy: copy.wait_send())


def trace_kernel(
    n_gx, n_gy, width, adjacent, coef, weights, own, packed_trace, packed_sums,
    applied, extended, returned, arrived, gathered, send_a, recv_a, send_b, recv_b,
):
    faces = own.shape[0]
    halo_len = (extended.shape[0] - faces) // packed_trace.shape[0]
    greet(n_gx, n_gy, False)
    first = Exchange(n_gx, n_gy, 1, packed_trace, arrived, send_a, recv_a)
    second = Exchange(n_gx, n_gy, -1, packed_sums, returned, send_b, recv_b)
    first.start()
    extended[:faces, :] = own[...]
    first.receive()
    second.start()
    unpack_all(arrived, width, extended, faces, halo_len)

    def finish(base, total):
        applied[pl.ds(base, TILE), :] = total

    apply_skeleton(adjacent, extended, coef, weights, gathered, finish)
    second.receive()
    first.finish()
    second.finish()


def residual_kernel(
    width, lists, owners, applied, collected, returned, residual, packed, sums, rows_back
):
    faces = applied.shape[0]
    halo_len = lists.shape[0] // packed.shape[0]
    sums[:faces, :] = collected[...] - applied[...]
    unpack_all(returned, width, rows_back, 0, halo_len)

    @pl.loop(0, lists.shape[0] // 16)
    def _(step):
        places = [owners[step * 16 + u] for u in range(16)]
        rows = [
            sums[pl.ds(places[u], 1), :] + rows_back[pl.ds(step * 16 + u, 1), :] for u in range(16)
        ]
        for u in range(16):
            sums[pl.ds(places[u], 1), :] = rows[u]

    residual[...] = sums[:faces, :]
    gather_rows(sums, lists, 0, rows_back, lists.shape[0])
    pack_all(rows_back, 0, halo_len, width, packed)


def line_copies(source, slots, size, here, device, send_sem, recv_sem):
    copies = []
    for r in range(1, size):
        copies.append(
            pltpu.make_async_remote_copy(
                src_ref=source,
                dst_ref=slots.at[here],
                send_sem=send_sem.at[r],
                recv_sem=recv_sem.at[r],
                device_id=device(lax.rem(here + r, size)),
                device_id_type=MESH,
            )
        )
        copies[-1].start()
    slots[here] = source[...]
    return copies


def line_sum(copies, slots, size):
    for item in copies:
        item.wait()
    result = slots[0]
    for s in range(1, size):
        result = result + slots[s]
    return result


def image_kernel(
    n_gx, n_gy, width, adjacent, slot, coef, weights, own, table, packed,
    total_out, picked_trace, picked_residual,
    arrived, extended, gathered, partial, middle, slots_y, slots_x,
    send_a, recv_a, send_y, recv_y, send_x, recv_x,
):
    faces = own.shape[0]
    half = width // 2
    halo_len = (extended.shape[0] - faces) // packed.shape[0]
    here_x, here_y = lax.axis_index("gx"), lax.axis_index("gy")
    greet(n_gx, n_gy, True)
    halo = Exchange(n_gx, n_gy, 1, packed, arrived, send_a, recv_a)
    halo.start()
    extended[:faces, :] = own[...]
    partial[...] = jnp.zeros_like(partial)
    count = picked_trace.shape[0]
    gather_rows(table, slot, 0, picked_trace, count)
    halo.receive()
    unpack_all(arrived, width, extended, faces, halo_len)
    lane = lax.broadcasted_iota(jnp.int32, (TILE, LANES), 1)

    def finish(base, total):
        res = extended[pl.ds(base, TILE), :]
        down = pltpu.roll(res, LANES - half, 1)
        up = pltpu.roll(res, half, 1)
        turned = jnp.where(lane < half, down, -up)
        partial[0:1, :] += jnp.sum(total * res, axis=0, keepdims=True)
        partial[1:2, :] += jnp.sum(total * turned, axis=0, keepdims=True)
        partial[2:3, :] += jnp.sum(total * total, axis=0, keepdims=True)

    apply_skeleton(adjacent, extended, coef, weights, gathered, finish)
    copies = line_copies(partial, slots_y, n_gy, here_y, lambda t: (here_x, t), send_y, recv_y)
    gather_rows(extended, slot, 0, picked_residual, count // 2)
    middle[...] = line_sum(copies, slots_y, n_gy)
    copies = line_copies(middle, slots_x, n_gx, here_x, lambda t: (t, here_y), send_x, recv_x)
    gather_rows(extended, slot, count // 2, picked_residual, count // 2)
    total_out[...] = line_sum(copies, slots_x, n_gx)
    halo.finish()


def local(
    n_gx, n_gy,
    vol_rhs, trace_in, pml_flag, stretch, cond_op, skel_op, block_coef, recon_op, lift_op,
    elem_face, adjacency, halo_list,
):
    f32 = jnp.float32
    faces = trace_in.shape[2]
    elems = vol_rhs.shape[2]
    half = trace_in.shape[1]
    rows = 2 * half
    neighbours = adjacency.shape[0]
    dirs, halo_len = halo_list.shape
    halo = dirs * halo_len
    shape = jax.ShapeDtypeStruct

    slot = elem_face.reshape(-1)
    flat_lists = halo_list.reshape(-1)
    lists = jnp.maximum(flat_lists, 0)
    owners = jnp.where(flat_lists >= 0, flat_lists, faces)
    adjacent = jnp.maximum(adjacency, 0).reshape(-1)
    live = jnp.concatenate([jnp.ones((1, faces), bool), adjacency >= 0], axis=0)
    coef = jnp.where(live[:, None], block_coef, 0.0).reshape(2 * (neighbours + 1), faces)
    coef = jnp.pad(coef.T, ((0, 0), (0, 16 - coef.shape[0])))

    blocks = jax.vmap(complex_block)(skel_op).transpose(0, 2, 1)
    weights = jnp.concatenate([pad_lanes(blocks), pad_lanes(times_i(blocks))], axis=-1)
    weights = jnp.pad(weights, ((0, 0), (0, LANES - rows), (0, 0)))
    high = lax.reduce_precision(weights, 8, 7)
    high, low = high.astype(jnp.bfloat16), (weights - high).astype(jnp.bfloat16)
    weights = jnp.stack([jnp.concatenate([w, w], axis=1) for w in (high, low)], axis=1)

    own = pad_lanes(trace_in.reshape(rows, faces).T)
    volume = vol_rhs.reshape(2 * vol_rhs.shape[1], elems)
    tilt = pml_flag.astype(f32) * stretch
    cond = jax.vmap(complex_block)(cond_op)
    cond = pad_lanes(cond.transpose(0, 2, 1))
    cond_i = pad_lanes(times_i(jax.vmap(complex_block)(cond_op).transpose(0, 2, 1)))

    def condense(matrix):
        return jnp.einsum(
            "ke,ikc->iec", volume, matrix, precision=lax.Precision.HIGHEST, preferred_element_type=f32
        )

    pieces = condense(cond) + tilt[None, :, None] * condense(cond_i)
    pieces = pieces.reshape(4 * elems, LANES)

    params = pltpu.CompilerParams(vmem_limit_bytes=BIG)
    table = pltpu.VMEM((faces + halo, LANES), f32)
    rows_shape = shape((faces, LANES), f32)
    packed_dims = (dirs, halo_len * rows // LANES, LANES)
    packed_shape = shape(packed_dims, f32)
    collected, packed_trace, packed_sums = pl.pallas_call(
        functools.partial(scatter_kernel, rows),
        out_shape=(rows_shape, packed_shape, packed_shape),
        in_specs=[SMEM, SMEM, VMEM, VMEM],
        out_specs=(VMEM,) * 3,
        scratch_shapes=[table] * 4,
        compiler_params=params,
    )(slot, lists, pieces, own)

    def talking(number):
        return pltpu.CompilerParams(
            collective_id=number, has_side_effects=True, vmem_limit_bytes=BIG
        )

    halo_sem = pltpu.SemaphoreType.DMA((dirs,))
    gathered = pltpu.VMEM((neighbours, TILE, LANES), f32)
    applied, extended, returned = pl.pallas_call(
        functools.partial(trace_kernel, n_gx, n_gy, rows),
        out_shape=(rows_shape, shape((faces + halo, LANES), f32), packed_shape),
        in_specs=[SMEM] + [VMEM] * 5,
        out_specs=(VMEM,) * 3,
        scratch_shapes=[pltpu.VMEM(packed_dims, f32), gathered] + [halo_sem] * 4,
        compiler_params=talking(0),
    )(adjacent, coef, weights, own, packed_trace, packed_sums)

    residual, packed = pl.pallas_call(
        functools.partial(residual_kernel, rows),
        out_shape=(rows_shape, packed_shape),
        in_specs=[SMEM] * 2 + [VMEM] * 3,
        out_specs=(VMEM, VMEM),
        scratch_shapes=[pltpu.VMEM((faces + 8, LANES), f32), pltpu.VMEM((halo, LANES), f32)],
        compiler_params=params,
    )(lists, owners, applied, collected, returned)

    tile = (8, LANES)
    picked_shape = shape((4 * elems, LANES), f32)
    total, picked_trace, picked_residual = pl.pallas_call(
        functools.partial(image_kernel, n_gx, n_gy, rows),
        out_shape=(shape(tile, f32), picked_shape, picked_shape),
        in_specs=[SMEM] * 2 + [VMEM] * 5,
        out_specs=(VMEM,) * 3,
        scratch_shapes=[
            pltpu.VMEM(packed_dims, f32), table, gathered,
            pltpu.VMEM(tile, f32), pltpu.VMEM(tile, f32),
            pltpu.VMEM((n_gy,) + tile, f32), pltpu.VMEM((n_gx,) + tile, f32),
        ]
        + [halo_sem] * 2
        + [pltpu.SemaphoreType.DMA((n_gy,))] * 2
        + [pltpu.SemaphoreType.DMA((n_gx,))] * 2,
        compiler_params=talking(1),
    )(adjacent, slot, coef, weights, residual, extended, packed)
    sums = jnp.sum(total, axis=1)
    step_real = sums[0] / sums[2]
    step_imag = sums[1] / sums[2]

    change = residual[:, :rows].T.reshape(2, half, faces)
    trace_out = trace_in + jnp.stack(
        [step_real * change[0] - step_imag * change[1], step_real * change[1] + step_imag * change[0]]
    )

    lift = jax.vmap(complex_block)(lift_op).transpose(0, 2, 1)
    lift_i = times_i(lift)
    lift_rows = jnp.pad(lift, ((0, 0), (0, LANES - rows), (0, 0)))
    lift_rows_i = jnp.pad(lift_i, ((0, 0), (0, LANES - rows), (0, 0)))

    def lifted(matrix, picked):
        return jnp.einsum(
            "icv,iec->ve", matrix, picked.reshape(4, elems, LANES),
            precision=lax.Precision.HIGHEST, preferred_element_type=f32,
        )

    stepped = step_real * lift_rows + step_imag * lift_rows_i
    base = jnp.dot(
        complex_block(recon_op), volume, precision=lax.Precision.HIGHEST, preferred_element_type=f32
    )
    mid = base.shape[0] // 2
    base = jnp.concatenate(
        [base[:mid] - tilt * base[mid:], base[mid:] + tilt * base[:mid]], axis=0
    )
    volume_out = base - lifted(lift_rows, picked_trace) - lifted(stepped, picked_residual)
    return trace_out, volume_out.reshape(vol_rhs.shape)


def solution(mesh):
    split_last = P(None, None, ("gx", "gy"))
    in_specs = (
        split_last, split_last, P(("gx", "gy")), P(("gx", "gy")), P(), P(), split_last, P(), P(),
        P(None, ("gx", "gy")), P(None, ("gx", "gy")), P(None, ("gx", "gy")),
    )
    return jax.shard_map(
        functools.partial(local, mesh.shape["gx"], mesh.shape["gy"]),
        mesh=mesh,
        in_specs=in_specs,
        out_specs=(split_last, split_last),
        check_vma=False,
    )
```

```python
import functools

import jax
import jax.numpy as jnp
from jax import lax
from jax.experimental import pallas as pl
from jax.experimental.pallas import tpu as pltpu
from jax.sharding import PartitionSpec as P

OFFSETS = ((-1, -1), (-1, 0), (-1, 1), (0, -1), (0, 1), (1, -1), (1, 0), (1, 1))
LANES = 128
TILE = 256
MESH = pl.DeviceIdType.MESH
VMEM = pl.BlockSpec(memory_space=pltpu.VMEM)
SMEM = pl.BlockSpec(memory_space=pltpu.SMEM)
BIG = 60 * 1024 * 1024


def complex_block(complex_pair):
    top_row = jnp.concatenate([complex_pair[0], -complex_pair[1]], axis=1)
    bottom_row = jnp.concatenate([complex_pair[1], complex_pair[0]], axis=1)
    return jnp.concatenate([top_row, bottom_row], axis=0)


def times_i(rows):
    half = rows.shape[-1] // 2
    return jnp.concatenate([-rows[..., half:], rows[..., :half]], axis=-1)


def pad_lanes(rows):
    return jnp.pad(rows, ((0, 0),) * (rows.ndim - 1) + ((0, LANES - rows.shape[-1]),))


def split(x):
    high = x.astype(jnp.bfloat16)
    return high, (x - high.astype(jnp.float32)).astype(jnp.bfloat16)


def gather_rows(source, index, index_base, target, count, group=32):
    @pl.loop(0, count // group)
    def _(step):
        base = step * group
        views = [index.at[pl.ds(index_base + base + first, 8)] for first in range(0, group, 8)]
        rows = [source[pl.ds(views[u // 8][u % 8], 1), :] for u in range(group)]
        for u in range(group):
            target[pl.ds(index_base + base + u, 1), :] = rows[u]


def pack(rows, width, target):
    half, extra = LANES // 2, width - LANES // 2
    count = rows.shape[0]
    mid, groups = count // 2, LANES // extra
    lane = lax.broadcasted_iota(jnp.int32, (mid, LANES), 1)
    target[:mid, :] = jnp.where(lane < half, rows[:mid], pltpu.roll(rows[mid:], half, 1))
    piece = count // groups
    small_lane = lax.broadcasted_iota(jnp.int32, (piece, LANES), 1)
    tail = jnp.zeros((piece, LANES), jnp.float32)
    for g in range(groups):
        part = rows[g * piece : (g + 1) * piece]
        shift = (g * extra - half) % LANES
        part = pltpu.roll(part, shift, 1) if shift else part
        tail = jnp.where((small_lane >= g * extra) & (small_lane < (g + 1) * extra), part, tail)
    target[mid:, :] = tail


def unpack(packed, width, count):
    half, extra = LANES // 2, width - LANES // 2
    mid, groups = count // 2, LANES // extra
    piece = count // groups
    front, tail = packed[:mid], packed[mid:]
    parts = []
    for g in range(groups):
        shift = (half - g * extra) % LANES
        parts.append(pltpu.roll(tail, shift, 1) if shift else tail)
    ends = jnp.concatenate(parts, axis=0)
    starts = jnp.concatenate([front, pltpu.roll(front, half, 1)], axis=0)
    lane = lax.broadcasted_iota(jnp.int32, (count, LANES), 1)
    return jnp.where(lane < half, starts, jnp.where(lane < width, ends, 0.0))


def pack_all(source, first, halo_len, width, target):
    @pl.loop(0, target.shape[0])
    def _(d):
        base = pl.multiple_of(first + d * halo_len, 8)
        pack(source[pl.ds(base, halo_len), :], width, target.at[d])


def unpack_all(source, width, target, first, halo_len):
    @pl.loop(0, source.shape[0])
    def _(d):
        base = pl.multiple_of(first + d * halo_len, 8)
        target[pl.ds(base, halo_len), :] = unpack(source[d], width, halo_len)


def scatter_kernel(
    width, slot, lists, pieces, own, collected, packed_trace, packed_sums, total, part1, part2, part3
):
    count = pieces.shape[0] // 4
    faces = own.shape[0]
    halo_len = lists.shape[0] // packed_trace.shape[0]
    gather_rows(own, lists, 0, total, lists.shape[0])
    pack_all(total, 0, halo_len, width, packed_trace)
    parts = (total, part1, part2, part3)
    for part in parts:
        part[...] = jnp.zeros_like(part)

    @pl.loop(0, count // 8)
    def _(step):
        for u in range(8):
            e = step * 8 + u
            places = [slot[corner * count + e] for corner in range(4)]
            sums = [
                parts[corner][pl.ds(places[corner], 1), :] + pieces[pl.ds(corner * count + e, 1), :]
                for corner in range(4)
            ]
            for corner in range(4):
                parts[corner][pl.ds(places[corner], 1), :] = sums[corner]

    def joined(rows):
        return (total[rows, :] + part1[rows, :]) + (part2[rows, :] + part3[rows, :])

    @pl.loop(0, faces // TILE)
    def _(step):
        rows = pl.ds(pl.multiple_of(step * TILE, TILE), TILE)
        collected[rows, :] = joined(rows)

    @pl.loop(0, packed_sums.shape[0])
    def _(d):
        rows = pl.ds(pl.multiple_of(faces + d * halo_len, 8), halo_len)
        pack(joined(rows), width, packed_sums.at[d])


def apply_skeleton(adjacent, extended, coef, weights, gathered, finish):
    faces = coef.shape[0]
    neighbours = gathered.shape[0]

    @pl.loop(0, faces // TILE)
    def _(step):
        base = pl.multiple_of(step * TILE, TILE)

        @pl.loop(0, TILE // 8)
        def _(group):
            first = group * 8
            for k in range(neighbours):
                view = adjacent.at[pl.ds(k * faces + base + first, 8)]
                rows = [extended[pl.ds(view[u], 1), :] for u in range(8)]
                for u in range(8):
                    gathered[k, pl.ds(first + u, 1), :] = rows[u]

        scale = coef[pl.ds(base, TILE), :]
        total = None
        for k in range(neighbours + 1):
            x = extended[pl.ds(base, TILE), :] if k == 0 else gathered[k - 1]
            both = jnp.concatenate(split(x), axis=1)
            y = jnp.dot(both, weights[k, 0], preferred_element_type=jnp.float32)
            y += jnp.dot(both, weights[k, 1], preferred_element_type=jnp.float32)
            term = scale[:, 2 * k : 2 * k + 1] * y[:, :LANES] + scale[:, 2 * k + 1 : 2 * k + 2] * y[:, LANES:]
            total = term if total is None else total + term
        finish(base, total)


def inside(n_gx, n_gy, off, sign):
    x, y = lax.axis_index("gx") + sign * off[0], lax.axis_index("gy") + sign * off[1]
    return (x >= 0) & (x < n_gx) & (y >= 0) & (y < n_gy)


def greet(n_gx, n_gy, lines):
    here_x, here_y = lax.axis_index("gx"), lax.axis_index("gy")
    barrier = pltpu.get_barrier_semaphore()
    peers = 0
    for off in OFFSETS:

        @pl.when(inside(n_gx, n_gy, off, 1))
        def _():
            pl.semaphore_signal(
                barrier, inc=1, device_id=(here_x + off[0], here_y + off[1]), device_id_type=MESH
            )

        peers = peers + inside(n_gx, n_gy, off, 1).astype(jnp.int32)
    if lines:
        for r in range(1, n_gy):
            pl.semaphore_signal(
                barrier, inc=1, device_id=(here_x, lax.rem(here_y + r, n_gy)), device_id_type=MESH
            )
        for r in range(1, n_gx):
            pl.semaphore_signal(
                barrier, inc=1, device_id=(lax.rem(here_x + r, n_gx), here_y), device_id_type=MESH
            )
        peers = peers + (n_gx + n_gy - 2)
    pl.semaphore_wait(barrier, peers)


class Exchange:
    def __init__(self, n_gx, n_gy, sign, source, target, send_sem, recv_sem):
        self.grid, self.sign = (n_gx, n_gy), sign
        self.refs = source, target, send_sem, recv_sem

    def copy(self, d):
        source, target, send_sem, recv_sem = self.refs
        off, sign = OFFSETS[d], self.sign
        return pltpu.make_async_remote_copy(
            src_ref=source.at[d],
            dst_ref=target.at[d],
            send_sem=send_sem.at[d],
            recv_sem=recv_sem.at[d],
            device_id=(lax.axis_index("gx") + sign * off[0], lax.axis_index("gy") + sign * off[1]),
            device_id_type=MESH,
        )

    def each(self, sign, act):
        for d in range(len(OFFSETS)):

            @pl.when(inside(*self.grid, OFFSETS[d], sign))
            def _():
                act(self.copy(d))

    def start(self):
        self.each(self.sign, lambda copy: copy.start())

    def receive(self):
        self.each(-self.sign, lambda copy: copy.wait_recv())

    def finish(self):
        self.each(self.sign, lambda copy: copy.wait_send())


def trace_kernel(
    n_gx, n_gy, width, adjacent, coef, weights, own, packed_trace, packed_sums,
    applied, extended, returned, arrived, gathered, send_a, recv_a, send_b, recv_b,
):
    faces = own.shape[0]
    halo_len = (extended.shape[0] - faces) // packed_trace.shape[0]
    greet(n_gx, n_gy, False)
    first = Exchange(n_gx, n_gy, 1, packed_trace, arrived, send_a, recv_a)
    second = Exchange(n_gx, n_gy, -1, packed_sums, returned, send_b, recv_b)
    first.start()
    extended[:faces, :] = own[...]
    first.receive()
    second.start()
    unpack_all(arrived, width, extended, faces, halo_len)

    def finish(base, total):
        applied[pl.ds(base, TILE), :] = total

    apply_skeleton(adjacent, extended, coef, weights, gathered, finish)
    second.receive()
    first.finish()
    second.finish()


def residual_kernel(
    width, lists, owners, applied, collected, returned, residual, packed, sums, rows_back
):
    faces = applied.shape[0]
    halo_len = lists.shape[0] // packed.shape[0]
    sums[:faces, :] = collected[...] - applied[...]
    unpack_all(returned, width, rows_back, 0, halo_len)

    @pl.loop(0, lists.shape[0] // 16)
    def _(step):
        places = [owners[step * 16 + u] for u in range(16)]
        rows = [
            sums[pl.ds(places[u], 1), :] + rows_back[pl.ds(step * 16 + u, 1), :] for u in range(16)
        ]
        for u in range(16):
            sums[pl.ds(places[u], 1), :] = rows[u]

    residual[...] = sums[:faces, :]
    gather_rows(sums, lists, 0, rows_back, lists.shape[0])
    pack_all(rows_back, 0, halo_len, width, packed)


def line_copies(source, slots, size, here, device, send_sem, recv_sem):
    copies = []
    for r in range(1, size):
        copies.append(
            pltpu.make_async_remote_copy(
                src_ref=source,
                dst_ref=slots.at[here],
                send_sem=send_sem.at[r],
                recv_sem=recv_sem.at[r],
                device_id=device(lax.rem(here + r, size)),
                device_id_type=MESH,
            )
        )
        copies[-1].start()
    slots[here] = source[...]
    return copies


def line_sum(copies, slots, size):
    for item in copies:
        item.wait()
    result = slots[0]
    for s in range(1, size):
        result = result + slots[s]
    return result


def image_kernel(
    n_gx, n_gy, width, adjacent, slot, coef, weights, own, table, packed,
    change, picked_trace,
    picked_residual, arrived, extended, gathered, partial, middle, slots_y, slots_x,
    send_a, recv_a, send_y, recv_y, send_x, recv_x,
):
    faces = own.shape[0]
    half = width // 2
    halo_len = (extended.shape[0] - faces) // packed.shape[0]
    here_x, here_y = lax.axis_index("gx"), lax.axis_index("gy")
    greet(n_gx, n_gy, True)
    halo = Exchange(n_gx, n_gy, 1, packed, arrived, send_a, recv_a)
    halo.start()
    extended[:faces, :] = own[...]
    partial[...] = jnp.zeros_like(partial)
    count = picked_trace.shape[0]
    gather_rows(table, slot, 0, picked_trace, count)
    halo.receive()
    unpack_all(arrived, width, extended, faces, halo_len)
    lane = lax.broadcasted_iota(jnp.int32, (TILE, LANES), 1)

    def finish(base, total):
        res = extended[pl.ds(base, TILE), :]
        down = pltpu.roll(res, LANES - half, 1)
        up = pltpu.roll(res, half, 1)
        turned = jnp.where(lane < half, down, -up)
        partial[0:1, :] += jnp.sum(total * res, axis=0, keepdims=True)
        partial[1:2, :] += jnp.sum(total * turned, axis=0, keepdims=True)
        partial[2:3, :] += jnp.sum(total * total, axis=0, keepdims=True)

    apply_skeleton(adjacent, extended, coef, weights, gathered, finish)
    copies = line_copies(partial, slots_y, n_gy, here_y, lambda t: (here_x, t), send_y, recv_y)
    gather_rows(extended, slot, 0, picked_residual, count // 2)
    middle[...] = line_sum(copies, slots_y, n_gy)
    copies = line_copies(middle, slots_x, n_gx, here_x, lambda t: (t, here_y), send_x, recv_x)
    gather_rows(extended, slot, count // 2, picked_residual, count // 2)
    sums = jnp.sum(line_sum(copies, slots_x, n_gx), axis=1, keepdims=True)
    step_real = jnp.broadcast_to(sums[0:1] / sums[2:3], (TILE, LANES))
    step_imag = jnp.broadcast_to(sums[1:2] / sums[2:3], (TILE, LANES))

    def stepped(x):
        turned = jnp.where(lane < half, -pltpu.roll(x, LANES - half, 1), pltpu.roll(x, half, 1))
        return step_real * x + step_imag * turned

    @pl.loop(0, faces // TILE)
    def _(step):
        rows = pl.ds(pl.multiple_of(step * TILE, TILE), TILE)
        change[rows, :] = stepped(extended[rows, :])

    @pl.loop(0, count // TILE)
    def _(step):
        rows = pl.ds(pl.multiple_of(step * TILE, TILE), TILE)
        picked_trace[rows, :] = picked_trace[rows, :] + stepped(picked_residual[rows, :])

    halo.finish()


def local(
    n_gx, n_gy,
    vol_rhs, trace_in, pml_flag, stretch, cond_op, skel_op, block_coef, recon_op, lift_op,
    elem_face, adjacency, halo_list,
):
    f32 = jnp.float32
    faces = trace_in.shape[2]
    elems = vol_rhs.shape[2]
    half = trace_in.shape[1]
    rows = 2 * half
    neighbours = adjacency.shape[0]
    dirs, halo_len = halo_list.shape
    halo = dirs * halo_len
    shape = jax.ShapeDtypeStruct

    slot = elem_face.reshape(-1)
    flat_lists = halo_list.reshape(-1)
    lists = jnp.maximum(flat_lists, 0)
    owners = jnp.where(flat_lists >= 0, flat_lists, faces)
    adjacent = jnp.maximum(adjacency, 0).reshape(-1)
    live = jnp.concatenate([jnp.ones((1, faces), bool), adjacency >= 0], axis=0)
    coef = jnp.where(live[:, None], block_coef, 0.0).reshape(2 * (neighbours + 1), faces)
    coef = jnp.pad(coef.T, ((0, 0), (0, 16 - coef.shape[0])))

    blocks = jax.vmap(complex_block)(skel_op).transpose(0, 2, 1)
    weights = jnp.concatenate([pad_lanes(blocks), pad_lanes(times_i(blocks))], axis=-1)
    weights = jnp.pad(weights, ((0, 0), (0, LANES - rows), (0, 0)))
    high = lax.reduce_precision(weights, 8, 7)
    high, low = high.astype(jnp.bfloat16), (weights - high).astype(jnp.bfloat16)
    weights = jnp.stack([jnp.concatenate([w, w], axis=1) for w in (high, low)], axis=1)

    own = pad_lanes(trace_in.reshape(rows, faces).T)
    volume = vol_rhs.reshape(2 * vol_rhs.shape[1], elems)
    tilt = pml_flag.astype(f32) * stretch
    cond = jax.vmap(complex_block)(cond_op)
    cond = pad_lanes(cond.transpose(0, 2, 1))
    cond_i = pad_lanes(times_i(jax.vmap(complex_block)(cond_op).transpose(0, 2, 1)))

    def condense(matrix):
        return jnp.einsum(
            "ke,ikc->iec", volume, matrix, precision=lax.Precision.HIGHEST, preferred_element_type=f32
        )

    pieces = condense(cond) + tilt[None, :, None] * condense(cond_i)
    pieces = pieces.reshape(4 * elems, LANES)

    params = pltpu.CompilerParams(vmem_limit_bytes=BIG)
    table = pltpu.VMEM((faces + halo, LANES), f32)
    rows_shape = shape((faces, LANES), f32)
    packed_dims = (dirs, halo_len * rows // LANES, LANES)
    packed_shape = shape(packed_dims, f32)
    collected, packed_trace, packed_sums = pl.pallas_call(
        functools.partial(scatter_kernel, rows),
        out_shape=(rows_shape, packed_shape, packed_shape),
        in_specs=[SMEM, SMEM, VMEM, VMEM],
        out_specs=(VMEM,) * 3,
        scratch_shapes=[table] * 4,
        compiler_params=params,
    )(slot, lists, pieces, own)

    def talking(number):
        return pltpu.CompilerParams(
            collective_id=number, has_side_effects=True, vmem_limit_bytes=BIG
        )

    halo_sem = pltpu.SemaphoreType.DMA((dirs,))
    gathered = pltpu.VMEM((neighbours, TILE, LANES), f32)
    applied, extended, returned = pl.pallas_call(
        functools.partial(trace_kernel, n_gx, n_gy, rows),
        out_shape=(rows_shape, shape((faces + halo, LANES), f32), packed_shape),
        in_specs=[SMEM] + [VMEM] * 5,
        out_specs=(VMEM,) * 3,
        scratch_shapes=[pltpu.VMEM(packed_dims, f32), gathered] + [halo_sem] * 4,
        compiler_params=talking(0),
    )(adjacent, coef, weights, own, packed_trace, packed_sums)

    residual, packed = pl.pallas_call(
        functools.partial(residual_kernel, rows),
        out_shape=(rows_shape, packed_shape),
        in_specs=[SMEM] * 2 + [VMEM] * 3,
        out_specs=(VMEM, VMEM),
        scratch_shapes=[pltpu.VMEM((faces + 8, LANES), f32), pltpu.VMEM((halo, LANES), f32)],
        compiler_params=params,
    )(lists, owners, applied, collected, returned)

    tile = (8, LANES)
    picked_shape = shape((4 * elems, LANES), f32)
    change, picked = pl.pallas_call(
        functools.partial(image_kernel, n_gx, n_gy, rows),
        out_shape=(rows_shape, picked_shape),
        in_specs=[SMEM] * 2 + [VMEM] * 5,
        out_specs=(VMEM,) * 2,
        scratch_shapes=[
            pltpu.VMEM((4 * elems, LANES), f32),
            pltpu.VMEM(packed_dims, f32), table, gathered,
            pltpu.VMEM(tile, f32), pltpu.VMEM(tile, f32),
            pltpu.VMEM((n_gy,) + tile, f32), pltpu.VMEM((n_gx,) + tile, f32),
        ]
        + [halo_sem] * 2
        + [pltpu.SemaphoreType.DMA((n_gy,))] * 2
        + [pltpu.SemaphoreType.DMA((n_gx,))] * 2,
        compiler_params=talking(1),
    )(adjacent, slot, coef, weights, residual, extended, packed)
    trace_out = trace_in + change[:, :rows].T.reshape(trace_in.shape)

    lift = jax.vmap(complex_block)(lift_op).transpose(0, 2, 1)
    lift_rows = jnp.pad(lift, ((0, 0), (0, LANES - rows), (0, 0)))

    def lifted(matrix, picked):
        return jnp.einsum(
            "icv,iec->ve", matrix, picked.reshape(4, elems, LANES),
            precision=lax.Precision.HIGHEST, preferred_element_type=f32,
        )

    base = jnp.dot(
        complex_block(recon_op), volume, precision=lax.Precision.HIGHEST, preferred_element_type=f32
    )
    mid = base.shape[0] // 2
    base = jnp.concatenate(
        [base[:mid] - tilt * base[mid:], base[mid:] + tilt * base[:mid]], axis=0
    )
    volume_out = base - lifted(lift_rows, picked)
    return trace_out, volume_out.reshape(vol_rhs.shape)


def solution(mesh):
    split_last = P(None, None, ("gx", "gy"))
    in_specs = (
        split_last, split_last, P(("gx", "gy")), P(("gx", "gy")), P(), P(), split_last, P(), P(),
        P(None, ("gx", "gy")), P(None, ("gx", "gy")), P(None, ("gx", "gy")),
    )
    return jax.shard_map(
        functools.partial(local, mesh.shape["gx"], mesh.shape["gy"]),
        mesh=mesh,
        in_specs=in_specs,
        out_specs=(split_last, split_last),
        check_vma=False,
    )
```
